32 devices in a mesh: row: 8 (over y, x, core), col: 4 (over z).
Axes of the slice: x: 2, y: 2, z: 4, core: 2. Of those that a mesh axis runs over, the one named last changes fastest.
Arguments:
- thin_line_values: float32 [1024, 65536], P('row', 'col'), may hold values from 0 to 65520, as said below
- occupied_patch_flags: int32 [8, 512], P('row', 'col'), may hold values 0 or 1
- leader_vertical_patch: int32 [2], replicated, may hold values from 0 to 511, as said below
- leader_square_lines: float32 [2, 128, 65536], P(None, 'row', 'col'), may hold values from 0 to 65520, as said below
- leader_square_reciprocals: float32 [2, 128, 128], replicated, may hold values from 0 to 65520, as said below
- remaining_destination_line: int32 [1024], P('row'), may hold values from 0 to 7, as said below
- leading_square_lines: float32 [512, 65536], P('row', 'col'), may hold values from 0 to 65520, as said below
- leading_square_reciprocal: float32 [512, 512], replicated, may hold values from 0 to 65520, as said below
Outputs:
- dense_grid: float32 [1024, 65536], P('row', 'col')
The draws below stay inside these ranges and needn't reach their ends.
Inputs may be any that keep to these rules, and one draw needn't show every extreme that they name: `leader_vertical_patch`: distinct column tiles; the last column tile is among them. `remaining_destination_line`: among the rows of one index of row no value appears more than 16 times; one value, the same for every index of row, appears exactly 16 times in each. `thin_line_values`: Integers. `leader_square_lines`: Integers. `leader_square_reciprocals`: Integers. `leading_square_lines`: Integers. `leading_square_reciprocal`: Integers.
All inputs are finite; a program needn't handle non-finite values. No bound on the sum of `occupied_patch_flags` on one device may be relied on, other than what follows from the above.
Results may differ from the reference program's by a relative error of at most 0.0003.
Values sent between devices are 32-bit elements; how exact they have to be, the bound alone decides.
No kernel may reach another device: no remote copies, remote signals or barrier semaphores. Data moves between devices by JAX's collectives and lax.ppermute only.
A program may use at most 256 MiB of HBM per device.

```python
import jax
import jax.numpy as jnp
from jax import lax

TILE = 128
PANEL = 512
WIN = 65536
NPIV = 2
THIN_LINES_EACH = 128
MAX_PER_DEST = 16
SROWS = 1024
DROWS = 1024
N_ROW = 8
N_COL = 4


def residue_block(key, shape):
    uniform_part = jax.random.uniform(key, shape, jnp.float32)
    values = jnp.minimum(jnp.floor(uniform_part * 65521.0), 65520.0)
    return values


def draw_thin_line_values(key, part):
    return residue_block(jax.random.fold_in(key, 11), (SROWS, WIN))


def draw_leader_square_lines(key, part):
    return residue_block(jax.random.fold_in(key, 12), (NPIV, TILE, WIN))


def draw_leader_square_reciprocals(key, part):
    return residue_block(jax.random.fold_in(key, 13), (NPIV, TILE, TILE))


def draw_leading_square_lines(key, part):
    return residue_block(jax.random.fold_in(key, 14), (PANEL, WIN))


def draw_leading_square_reciprocal(key, part):
    return residue_block(jax.random.fold_in(key, 15), (PANEL, PANEL))


def draw_leader_vertical_patch(key, part):
    shuffled = jax.random.permutation(jax.random.fold_in(key, 16), WIN // TILE - 1).astype(jnp.int32)
    listed = jnp.concatenate([jnp.full((1,), WIN // TILE - 1, jnp.int32), shuffled[:NPIV - 1]])
    return jax.random.permutation(jax.random.fold_in(key, 18), listed).astype(jnp.int32)


def draw_remaining_destination_line(key, part):
    base_key = jax.random.fold_in(key, 17)
    hottest = jax.random.randint(jax.random.fold_in(base_key, 1), (), 0, N_ROW).astype(jnp.int32)
    slot_dest = jnp.repeat(jnp.arange(N_ROW, dtype=jnp.int32), MAX_PER_DEST)

    def sender(sender_index):
        sender_key = jax.random.fold_in(base_key, sender_index + 100)
        shuffled = jax.random.permutation(jax.random.fold_in(sender_key, 1), N_ROW * MAX_PER_DEST).astype(jnp.int32)
        scores = (slot_dest == hottest).astype(jnp.int32) * (N_ROW * MAX_PER_DEST) + shuffled
        order = jnp.argsort(scores)
        chosen = slot_dest[order[:THIN_LINES_EACH - MAX_PER_DEST]]
        whole = jnp.concatenate([jnp.full((MAX_PER_DEST,), hottest, jnp.int32), chosen])
        return jax.random.permutation(jax.random.fold_in(sender_key, 2), whole)
    return jax.vmap(sender)(jnp.arange(N_ROW, dtype=jnp.int32)).reshape(SROWS).astype(jnp.int32)


def set_ends(drawn, own_key, least, largest):
    extent = drawn.shape
    place = [jax.random.randint(jax.random.fold_in(own_key, axis), (), 0, extent[axis]) for axis in range(len(extent))]
    drawn = drawn.at[tuple(place)].set(least)
    longest = extent.index(max(extent))
    place[longest] = (place[longest] + 1) % extent[longest]
    return drawn.at[tuple(place)].set(largest)


def setup_inputs(seed: int = 0) -> dict:
    key_of = jax.random.split(jax.random.key(seed), 9)
    return {
        "thin_line_values": draw_thin_line_values(jax.random.fold_in(key_of[8], 71), 0),
        "occupied_patch_flags": set_ends((jax.random.randint(key_of[1], (SROWS // TILE, WIN // TILE), 0, 2) < 1).astype(jnp.int32), jax.random.fold_in(key_of[1], 1), 0, 1),
        "leader_vertical_patch": draw_leader_vertical_patch(jax.random.fold_in(key_of[8], 71), 0),
        "leader_square_lines": draw_leader_square_lines(jax.random.fold_in(key_of[8], 71), 0),
        "leader_square_reciprocals": draw_leader_square_reciprocals(jax.random.fold_in(key_of[8], 71), 0),
        "remaining_destination_line": draw_remaining_destination_line(jax.random.fold_in(key_of[8], 71), 0),
        "leading_square_lines": draw_leading_square_lines(jax.random.fold_in(key_of[8], 71), 0),
        "leading_square_reciprocal": draw_leading_square_reciprocal(jax.random.fold_in(key_of[8], 71), 0),
    }


modulus = 65521.0


def reduce_mod(values):
    quotient = jnp.floor(values / modulus)
    remain = values - quotient * modulus
    remain = jnp.where(remain < 0.0, remain + modulus, remain)
    return jnp.where(remain >= modulus, remain - modulus, remain)


def split_limbs(values):
    upper = jnp.floor(values / 256.0)
    return upper, values - upper * 256.0


def mat_dot(left, right):
    return jnp.dot(left, right, preferred_element_type=jnp.float32, precision=lax.Precision.HIGHEST)


def mul_mod(left, right):
    left_hi, left_lo = split_limbs(left)
    right_hi, right_lo = split_limbs(right)
    total = jnp.zeros((left.shape[0], right.shape[1]), jnp.float32)
    for offset in range(0, left.shape[1], 128):
        a_hi = left_hi[:, offset:offset + 128]
        a_lo = left_lo[:, offset:offset + 128]
        b_hi = right_hi[offset:offset + 128]
        b_lo = right_lo[offset:offset + 128]
        high = mat_dot(a_hi, b_hi)
        cross = mat_dot(a_hi, b_lo) + mat_dot(a_lo, b_hi)
        low = mat_dot(a_lo, b_lo)
        part = reduce_mod(reduce_mod(cross) * 256.0) + reduce_mod(high) * 15.0 + reduce_mod(low)
        total = reduce_mod(total + part)
    return total


def reference(thin_line_values, occupied_patch_flags, leader_vertical_patch, leader_square_lines, leader_square_reciprocals, remaining_destination_line, leading_square_lines, leading_square_reciprocal):
    pattern = occupied_patch_flags.astype(jnp.float32)

    def masked_columns(begin, width):
        rows_part = lax.dynamic_slice_in_dim(thin_line_values, begin, width, 1)
        tiles_part = lax.dynamic_slice_in_dim(pattern, begin // TILE, width // TILE, 1)
        expanded = jnp.repeat(jnp.repeat(tiles_part, TILE, 0), TILE, 1)
        return rows_part * expanded

    factors = []
    for pivot in range(NPIV):
        column = (leader_vertical_patch[pivot] * TILE).astype(jnp.int32)
        tile_now = masked_columns(column, TILE)
        for earlier in range(pivot):
            prior = lax.dynamic_slice_in_dim(leader_square_lines[earlier], column, TILE, 1)
            tile_now = reduce_mod(tile_now - mul_mod(factors[earlier], prior))
        factors.append(mul_mod(tile_now, leader_square_reciprocals[pivot]))

    bucketed_lines = remaining_destination_line.reshape(N_ROW, THIN_LINES_EACH)
    indicator_matrix = (bucketed_lines[:, :, None] == jnp.arange(N_ROW, dtype=jnp.int32)[None, None, :]).astype(jnp.int32)
    landing_order = jnp.sum((jnp.cumsum(indicator_matrix, axis=1) - 1) * indicator_matrix, axis=2)
    sources = jnp.arange(N_ROW, dtype=jnp.int32)[:, None]
    target = (bucketed_lines * (N_ROW * MAX_PER_DEST) + sources * MAX_PER_DEST + landing_order).reshape(SROWS).astype(jnp.int32)

    def gridded_columns(begin, width):
        eliminated_lines = masked_columns(begin, width)
        for pivot in range(NPIV):
            block = lax.dynamic_slice_in_dim(leader_square_lines[pivot], begin, width, 1)
            eliminated_lines = reduce_mod(eliminated_lines - mul_mod(factors[pivot], block))
        return jnp.zeros((DROWS, width), jnp.float32).at[target].set(eliminated_lines)

    lower = mul_mod(gridded_columns(jnp.int32(0), PANEL), leading_square_reciprocal)
    block_width = WIN // N_COL

    def finish(block_index):
        begin = (block_index * block_width).astype(jnp.int32)
        patchwise_arrangement = gridded_columns(begin, block_width)
        strip = lax.dynamic_slice_in_dim(leading_square_lines, begin, block_width, 1)
        return reduce_mod(patchwise_arrangement - mul_mod(lower, strip)) / modulus

    blocks = lax.map(finish, jnp.arange(N_COL, dtype=jnp.int32))
    return jnp.transpose(blocks, (1, 0, 2)).reshape(DROWS, WIN)
```

```python
import functools

import jax
import jax.numpy as jnp
from jax import lax
from jax.experimental import pallas as pl
from jax.experimental.pallas import tpu as pltpu
from jax.sharding import PartitionSpec as P

TILE = 128
PANEL = 512
NPIV = 2
MAX_PER_DEST = 16
MODULUS = 65521.0
INVERSE = 1.0 / MODULUS
MAGIC = 12582912.0
CHUNKS = 4
WIDE = 512


def rounded(x):
    return (x + MAGIC) - MAGIC


def centred(x):
    return x - MODULUS * rounded(x * INVERSE)


def limbs(x):
    high = rounded(x * (1.0 / 256.0))
    return high, x - 256.0 * high


def bf16_limbs(x):
    high, low = limbs(x)
    return high.astype(jnp.bfloat16), low.astype(jnp.bfloat16)


def dot(a, b):
    return jnp.dot(a, b, preferred_element_type=jnp.float32)


def folded(x):
    quotient = rounded(x * (1.0 / 256.0))
    return 15.0 * quotient + 256.0 * (x - 256.0 * quotient)


def mul_mod(left, right):
    ah, al = bf16_limbs(left)
    bh, bl = bf16_limbs(right)
    high = centred(dot(ah, bh))
    cross = dot(jnp.concatenate([ah, al], axis=1), jnp.concatenate([bl, bh], axis=0))
    return centred(15.0 * high + folded(cross) + dot(al, bl))


def near_zero(x):
    return jnp.where(x > 32760.0, x - MODULUS, x)


def span(bits):
    masks = [0]
    for bit in bits:
        masks = masks + [m | bit for m in masks]
    return sorted(masks)


class Role:
    def __init__(self, first, second):
        self.first = first
        self.second = second
        self.gathered = span([1] + first)
        self.reduced = span([1] + second)


def call(kernel, name, grid, inputs, in_specs, outputs, out_specs, scratch=(), prefetch=0, aliases=None, cost=None, vmem=None):
    flops, moved = cost or (0, 0)
    return pl.pallas_call(
        kernel,
        name=name,
        out_shape=outputs,
        grid_spec=pltpu.PrefetchScalarGridSpec(
            num_scalar_prefetch=prefetch,
            grid=grid,
            in_specs=in_specs,
            out_specs=out_specs,
            scratch_shapes=list(scratch),
        ),
        input_output_aliases=aliases or {},
        compiler_params=pltpu.CompilerParams(
            dimension_semantics=("arbitrary",) * len(grid), vmem_limit_bytes=vmem or 48 * 1024 * 1024
        ),
        cost_estimate=pl.CostEstimate(flops=flops, bytes_accessed=moved, transcendentals=0),
    )(*inputs)


def f32(*shape):
    return jax.ShapeDtypeStruct(shape, jnp.float32)


def prepare_kernel(slots, pos, tiles, dest, t0, t1, tp, m0, m1, mp, l0, l1, lp, order_out, near_out, panel_out):
    rows = dest.shape[1]
    mine = pos[0]
    to_row = dest[...] ^ mine
    across = jnp.broadcast_to(to_row.astype(jnp.float32), (rows, rows))
    down = across.T
    earlier = lax.broadcasted_iota(jnp.int32, (rows, rows), 0) < lax.broadcasted_iota(jnp.int32, (rows, rows), 1)
    before = jnp.where((across == down) & earlier, 1.0, 0.0)
    landing = jnp.sum(before, axis=0, keepdims=True)
    place = to_row * MAX_PER_DEST + landing.astype(jnp.int32)
    choose = lax.broadcasted_iota(jnp.int32, (slots, rows), 0) == place
    order = jnp.where(choose, 1.0, 0.0).astype(jnp.bfloat16)
    order_out[...] = order

    def placed(block):
        high, low = bf16_limbs(block)
        return 256.0 * dot(order, high) + dot(order, low)

    lrows = 2 * l0.shape[1]
    near_out[:slots, :TILE] = placed(t0[...] * m0[...])
    near_out[:slots, TILE:] = placed(t1[...] * m1[...])
    near_out[slots:, :TILE] = l0[...].reshape(lrows, TILE)
    near_out[slots:, TILE:] = l1[...].reshape(lrows, TILE)
    panel_out[:slots, :] = placed(tp[...] * mp[...])
    panel_out[slots:, :] = lp[...].reshape(lrows, PANEL)


def prepare(pos, tiles, dest, thin, mask, leads, slots):
    rows, width = thin.shape
    per = width // TILE
    lper = leads.shape[1]
    total = slots + 2 * lper
    tile = lambda k: (lambda i, pos, tiles: (0, lax.rem(tiles[k], per)))
    tile3 = lambda k: (lambda i, pos, tiles: (0, 0, lax.rem(tiles[k], per)))
    zero = lambda i, pos, tiles: (0, 0)
    zero3 = lambda i, pos, tiles: (0, 0, 0)
    return call(
        functools.partial(prepare_kernel, slots),
        "prepare",
        (1,),
        (pos, tiles, dest, thin, thin, thin, mask, mask, mask, leads, leads, leads),
        [
            pl.BlockSpec((1, rows), zero),
            pl.BlockSpec((rows, TILE), tile(0)),
            pl.BlockSpec((rows, TILE), tile(1)),
            pl.BlockSpec((rows, PANEL), zero),
            pl.BlockSpec((1, TILE), tile(0)),
            pl.BlockSpec((1, TILE), tile(1)),
            pl.BlockSpec((1, PANEL), zero),
            pl.BlockSpec((2, lper, TILE), tile3(0)),
            pl.BlockSpec((2, lper, TILE), tile3(1)),
            pl.BlockSpec((2, lper, PANEL), zero3),
        ],
        (jax.ShapeDtypeStruct((slots, rows), jnp.bfloat16), f32(total, 2 * TILE), f32(total, PANEL)),
        (
            pl.BlockSpec((slots, rows), zero),
            pl.BlockSpec((total, 2 * TILE), zero),
            pl.BlockSpec((total, PANEL), zero),
        ),
        prefetch=2,
        cost=(2 * slots * rows * 768 * 2, 4 * total * 768 * 2),
    )


def choose_kernel(cols, per, half, pos, tiles, *refs):
    near, panel, (first, second) = refs[:cols], refs[cols : 2 * cols], refs[2 * cols :]
    here = pos[1]

    def chosen(parts, owner):
        value = parts[0]
        for mask in range(1, len(parts)):
            value = jnp.where((owner ^ here) == mask, parts[mask], value)
        return value

    for k in range(2):
        columns = slice(k * TILE, (k + 1) * TILE)
        first[:, columns] = chosen([r[:, columns] for r in near], tiles[k] // per)
    rest = half - 2 * TILE
    first[:, 2 * TILE :] = chosen([r[:, :rest] for r in panel], 0)
    second[...] = chosen([r[:, rest:] for r in panel], 0)


def choose(pos, tiles, near, panel, per):
    cols = len(near)
    total = near[0].shape[0]
    half = (2 * TILE + PANEL) // 2
    zero = lambda i, pos, tiles: (0, 0)
    return call(
        functools.partial(choose_kernel, cols, per, half),
        "choose",
        (1,),
        (pos, tiles, *near, *panel),
        [pl.BlockSpec((total, 2 * TILE), zero)] * cols + [pl.BlockSpec((total, PANEL), zero)] * cols,
        (f32(total, half), f32(total, half)),
        (pl.BlockSpec((total, half), zero),) * 2,
        prefetch=2,
        cost=(0, 4 * total * 768 * (cols + 1)),
    )


def multiplier_kernel(n, roles, pos, *refs):
    x1, x1s, x2, x2s, g1, g1s, g2, g2s, reciprocals, lead = refs[:10]
    outs, (held, coefficient, lead_limbs) = refs[10:-3], refs[-3:]
    step = pl.program_id(0)
    mine = pos[0]
    slots = n * MAX_PER_DEST
    lper = TILE // n
    bits = n.bit_length() - 1

    @pl.when(step == 0)
    def _():
        for mask in range(n):
            plain, turned = mask >> 1, (mask >> 2) | (((mask >> 1) & 1) << (bits - 2))
            a = (g1s if mask & 1 else g1)[plain]
            b = (g2s if mask & 1 else g2)[turned]
            block = near_zero(jnp.concatenate([a, b], axis=1))
            at = pl.multiple_of((mine ^ mask) * lper, lper)
            for pivot in range(2):
                held[pivot, pl.ds(at, lper), :] = block[pivot * lper : (pivot + 1) * lper]
        high, low = bf16_limbs(near_zero(lead[...]))
        lead_limbs[0] = high
        lead_limbs[1] = low

    odd = (step & 1) == 1
    left = near_zero(jnp.where(odd, x1s[0], x1[0]))
    right = near_zero(jnp.where(odd, x2s[0], x2[0]))
    here = jnp.concatenate([left, right], axis=1)
    f0 = mul_mod(here[:, :TILE], near_zero(reciprocals[0]))
    changed = centred(here[:, TILE : 2 * TILE] - mul_mod(f0, held[0, :, TILE : 2 * TILE]))
    f1 = mul_mod(changed, near_zero(reciprocals[1]))
    both = jnp.concatenate([f0, f1], axis=1)
    panel_rows = jnp.concatenate([held[0, :, 2 * TILE :], held[1, :, 2 * TILE :]], axis=0)
    cleared = centred(here[:, 2 * TILE :] - mul_mod(both, panel_rows))
    ah, al = bf16_limbs(cleared)
    bh, bl = lead_limbs[0], lead_limbs[1]
    high = centred(dot(ah, bh))
    cross = dot(ah, bl) + dot(al, bh)
    lower = centred(15.0 * high + folded(cross) + dot(al, bl))
    coefficient[step, :, : 2 * TILE] = -both
    coefficient[step, :, 2 * TILE :] = -lower

    @pl.when(step == n - 1)
    def _():
        columns = 2 * TILE + PANEL
        sper = PANEL // n
        each = 2 * lper + sper
        for number, role in enumerate(roles):
            low_out, high_out, shift_out = outs[3 * number : 3 * number + 3]
            depth = len(role.gathered) * each
            at = lax.broadcasted_iota(jnp.int32, (columns, depth), 1)
            row = lax.broadcasted_iota(jnp.int32, (columns, depth), 0)
            wanted = jnp.zeros((columns, depth), jnp.int32)
            for k, mask in enumerate(role.gathered):
                inside = at - k * each
                owner = mine ^ mask
                source = jnp.where(
                    inside < lper,
                    owner * lper + inside,
                    jnp.where(
                        inside < 2 * lper,
                        TILE + owner * lper + (inside - lper),
                        2 * TILE + owner * sper + (inside - 2 * lper),
                    ),
                )
                wanted = jnp.where((inside >= 0) & (inside < each), source, wanted)
            select = jnp.where(row == wanted, 1.0, 0.0).astype(jnp.bfloat16)
            for k, e in enumerate(role.reduced):
                blocks = []
                for r in range(n):
                    rows = slice(r * MAX_PER_DEST, (r + 1) * MAX_PER_DEST)
                    blocks.append(coefficient[e ^ r, rows, :])
                value = jnp.concatenate(blocks, axis=0)
                high, low = bf16_limbs(value)
                scaled = centred(256.0 * value)
                scaled_high, scaled_low = bf16_limbs(scaled)
                place = slice(k * slots, (k + 1) * slots)
                picked_low, picked_high = dot(low, select), dot(high, select)
                low_out[place, :depth] = picked_low.astype(jnp.bfloat16)
                low_out[place, depth:] = dot(scaled_low, select).astype(jnp.bfloat16)
                high_out[place, :depth] = picked_high.astype(jnp.bfloat16)
                high_out[place, depth:] = dot(scaled_high, select).astype(jnp.bfloat16)
                total = jnp.sum(picked_low + 256.0 * picked_high, axis=1, keepdims=True)
                shift = centred(256.0 * centred(128.0 * centred(total)))
                shift_out[place, :] = jnp.broadcast_to(shift, (slots, TILE))


def multipliers(pos, n, roles, x1, x1s, x2, x2s, reciprocals, lead):
    slots = n * MAX_PER_DEST
    lper = TILE // n
    bits = n.bit_length() - 1
    half = (2 * TILE + PANEL) // 2
    each = 2 * lper + PANEL // n
    plain = lambda g, pos: (g >> 1, 0, 0)
    turned = lambda g, pos: ((g >> 2) | (((g >> 1) & 1) << (bits - 2)), 0, 0)
    lines = lambda g, pos: (0, slots // (2 * lper), 0)
    thin = lambda index: pl.BlockSpec((1, slots, half), index)
    lead_rows = pl.BlockSpec((n // 2, 2 * lper, half), lines)
    outputs, specs, flops = [], [], 0
    for role in roles:
        rows, depth = len(role.reduced) * slots, len(role.gathered) * each
        outputs += [
            jax.ShapeDtypeStruct((rows, 2 * depth), jnp.bfloat16),
            jax.ShapeDtypeStruct((rows, 2 * depth), jnp.bfloat16),
            f32(rows, TILE),
        ]
        specs += [pl.BlockSpec(o.shape, lambda g, pos: (0, 0)) for o in outputs[-3:]]
    out = call(
        functools.partial(multiplier_kernel, n, roles),
        "multipliers",
        (n,),
        (pos, x1, x1s, x2, x2s, x1, x1s, x2, x2s, reciprocals, lead),
        [thin(plain), thin(plain), thin(turned), thin(turned)]
        + [lead_rows] * 4
        + [
            pl.BlockSpec(reciprocals.shape, lambda g, pos: (0, 0, 0)),
            pl.BlockSpec(lead.shape, lambda g, pos: (0, 0)),
        ],
        tuple(outputs),
        tuple(specs),
        scratch=[
            pltpu.VMEM((2, TILE, 2 * TILE + PANEL), jnp.float32),
            pltpu.VMEM((n, slots, 2 * TILE + PANEL), jnp.float32),
            pltpu.VMEM((2, PANEL, PANEL), jnp.bfloat16),
        ],
        prefetch=1,
        cost=(8 * n * slots * PANEL * PANEL, 8 * n * slots * 768),
    )
    return [out[3 * k : 3 * k + 3] for k in range(len(roles))]


def pack_kernel(n, role, pos, order, thin, mask, leads, strip, *outs):
    lper, sper = leads.shape[1], strip.shape[0]
    high, low = bf16_limbs(thin[...] * mask[...])
    placed = 256.0 * dot(order[...], high) + dot(order[...], low)
    half = pl.program_id(0)
    for other in range(2):

        @pl.when(half == other)
        def _():
            for k, m in enumerate(role.gathered):
                if m & 1 != other:
                    continue
                out = outs[k]
                out[:lper, :] = leads[0]
                out[lper : 2 * lper, :] = leads[1]
                out[2 * lper : 2 * lper + sper, :] = strip[...]
                base = 2 * lper + sper
                for i, e in enumerate(role.reduced):
                    r = (e ^ m) * MAX_PER_DEST
                    at = base + i * MAX_PER_DEST
                    out[at : at + MAX_PER_DEST, :] = placed[r : r + MAX_PER_DEST]


def pack(pos, n, role, chunk, size, order, thin, mask, leads, strip):
    rows, lper, sper = thin.shape[0], leads.shape[1], strip.shape[0]
    slots = n * MAX_PER_DEST
    wide = min(WIDE, size)
    count = size // wide
    total = 2 * lper + sper + len(role.reduced) * MAX_PER_DEST
    column = lambda h, t, pos: (2 * chunk + ((pos[0] & 1) ^ h)) * count + t
    flat = lambda h, t, pos: (0, column(h, t, pos))
    deep = lambda h, t, pos: (0, 0, column(h, t, pos))
    index = (
        lambda h, t, pos: (0, jnp.where(h == 0, t, count - 1)),
        lambda h, t, pos: (0, jnp.where(h == 1, t, 0)),
    )
    return call(
        functools.partial(pack_kernel, n, role),
        f"pack_{chunk}",
        (2, count),
        (pos, order, thin, mask, leads, strip),
        [
            pl.BlockSpec((slots, rows), lambda h, t, pos: (0, 0)),
            pl.BlockSpec((rows, wide), flat),
            pl.BlockSpec((1, wide), flat),
            pl.BlockSpec((2, lper, wide), deep),
            pl.BlockSpec((sper, wide), flat),
        ],
        tuple(f32(total, size) for _ in role.gathered),
        tuple(pl.BlockSpec((total, wide), index[m & 1]) for m in role.gathered),
        prefetch=1,
        cost=(8 * slots * rows * size, 4 * size * (2 * (rows + 2 * lper + sper) + total * len(role.gathered))),
    )


def partial_kernel(n, role, each, low, high, shift, *refs):
    count = len(role.gathered)
    messages, outs = refs[:count], refs[count:]
    slots = n * MAX_PER_DEST
    lines = jnp.concatenate([m[:each, :] for m in messages], axis=0) - 32768.0
    line_high, line_low = bf16_limbs(lines)
    stacked = jnp.concatenate([line_low, line_high], axis=0)
    for k, e in enumerate(role.reduced):
        place = slice(k * slots, (k + 1) * slots)
        value = dot(low[place, :], stacked) + folded(dot(high[place, :], stacked)) + shift[place, :1]
        for r in range(n):
            rows = slice(r * MAX_PER_DEST, (r + 1) * MAX_PER_DEST)
            block = value[rows]
            if (r ^ e) in role.gathered:
                source = messages[role.gathered.index(r ^ e)]
                at = each + k * MAX_PER_DEST
                block = block + source[at : at + MAX_PER_DEST, :]
            outs[k][rows, :] = centred(block)


def partial_sums(n, role, chunk, matrices, messages):
    low, high, shift = matrices
    total, size = messages[0].shape
    slots = n * MAX_PER_DEST
    each = total - len(role.reduced) * MAX_PER_DEST
    wide = min(WIDE, size)
    fixed = lambda t: (0, 0)
    moving = lambda t: (0, t)
    return call(
        functools.partial(partial_kernel, n, role, each),
        f"partial_{chunk}",
        (size // wide,),
        (low, high, shift, *messages),
        [pl.BlockSpec(a.shape, fixed) for a in matrices] + [pl.BlockSpec((total, wide), moving)] * len(messages),
        tuple(f32(slots, size) for _ in role.reduced),
        tuple(pl.BlockSpec((slots, wide), moving) for _ in role.reduced),
        cost=(
            4 * low.shape[0] * low.shape[1] * size,
            4 * size * (total * len(messages) + slots * len(role.reduced)),
        ),
    )


def finish_kernel(n, role, pos, *refs):
    count = len(role.reduced)
    parts, out = refs[:count], refs[-1]
    half = pl.program_id(0)
    mine = pos[0]
    for other in range(2):

        @pl.when(half == other)
        def _():
            chosen = [part for part, e in zip(parts, role.reduced) if e & 1 == other]
            value = chosen[0][...]
            for part in chosen[1:]:
                value = value + part[...]
            value = centred(value)
            value = jnp.where(value < 0.0, value + MODULUS, value) * INVERSE
            for r in range(n):
                at = pl.multiple_of((mine ^ r) * MAX_PER_DEST, MAX_PER_DEST)
                out[pl.ds(at, MAX_PER_DEST), :] = value[r * MAX_PER_DEST : (r + 1) * MAX_PER_DEST]


def finish(pos, n, role, chunk, width, parts, so_far):
    slots, size = parts[0].shape
    wide = min(2 * WIDE, size)
    count = size // wide
    index = (
        lambda h, t, pos: (0, jnp.where(h == 0, t, count - 1)),
        lambda h, t, pos: (0, jnp.where(h == 1, t, 0)),
    )
    inputs, specs, aliases = [pos, *parts], [pl.BlockSpec((slots, wide), index[e & 1]) for e in role.reduced], {}
    if so_far is not None:
        aliases = {len(inputs): 0}
        inputs.append(so_far)
        specs.append(pl.BlockSpec(memory_space=pl.ANY))
    return call(
        functools.partial(finish_kernel, n, role),
        f"finish_{chunk}",
        (2, count),
        inputs,
        specs,
        f32(slots, width),
        pl.BlockSpec((slots, wide), lambda h, t, pos: (0, (2 * chunk + ((pos[0] & 1) ^ h)) * count + t)),
        prefetch=1,
        aliases=aliases,
        cost=(0, 4 * size * slots * (len(parts) + 2)),
    )


def exchange(value, axis, mask):
    size = lax.axis_size(axis)
    return lax.ppermute(value, axis, [(i, i ^ mask) for i in range(size)])


def local(
    thin_line_values,
    occupied_patch_flags,
    leader_vertical_patch,
    leader_square_lines,
    leader_square_reciprocals,
    remaining_destination_line,
    leading_square_lines,
    leading_square_reciprocal,
):
    n, cols = lax.axis_size("row"), lax.axis_size("col")
    rows, width = thin_line_values.shape
    slots = n * MAX_PER_DEST
    bits = [1 << k for k in range(1, n.bit_length() - 1)]
    roles = [Role(bits[:1], bits[1:]), Role(bits[1:], bits[:1])]
    pos = jnp.stack([lax.axis_index("row"), lax.axis_index("col")]).astype(jnp.int32)
    mask = jnp.broadcast_to(
        occupied_patch_flags.astype(jnp.float32)[:, :, None], (rows // TILE, width // TILE, TILE)
    ).reshape(rows // TILE, width)

    order, near, panel = prepare(
        pos,
        leader_vertical_patch,
        remaining_destination_line.reshape(1, rows),
        thin_line_values,
        mask,
        leader_square_lines,
        slots,
    )
    nears = [near] + [exchange(near, "col", m) for m in range(1, cols)]
    panels = [panel] + [lax.ppermute(panel, "col", [(0, m)]) for m in range(1, cols)]
    first, second = choose(pos, leader_vertical_patch, nears, panels, width // TILE)
    gathered = []
    for stack, steps in ((first[None], roles[0]), (second[None], roles[1])):
        for bit in steps.first + steps.second:
            stack = jnp.concatenate([stack, exchange(stack, "row", bit)], axis=0)
        gathered += [stack, exchange(stack, "row", 1)]
    matrices = multipliers(pos, n, roles, *gathered, leader_square_reciprocals, leading_square_reciprocal)

    size = width // (2 * CHUNKS)
    result = None
    for chunk in range(CHUNKS):
        role = roles[chunk % 2]
        packed = pack(
            pos, n, role, chunk, size, order, thin_line_values, mask, leader_square_lines, leading_square_lines
        )
        messages = [packed[0]] + [exchange(v, "row", m) for v, m in zip(packed[1:], role.gathered[1:])]
        sums = partial_sums(n, role, chunk, matrices[chunk % 2], messages)
        parts = [sums[0]] + [exchange(v, "row", e) for v, e in zip(sums[1:], role.reduced[1:])]
        result = finish(pos, n, role, chunk, width, parts, result)
    return result


def solution(mesh):
    return jax.shard_map(
        local,
        mesh=mesh,
        in_specs=(
            P("row", "col"),
            P("row", "col"),
            P(),
            P(None, "row", "col"),
            P(),
            P("row"),
            P("row", "col"),
            P(),
        ),
        out_specs=P("row", "col"),
        check_vma=False,
    )
```

```python
import functools

import jax
import jax.numpy as jnp
from jax import lax
from jax.experimental import pallas as pl
from jax.experimental.pallas import tpu as pltpu
from jax.sharding import PartitionSpec as P


TILE = 128
PANEL = 512
MAX_PER_DEST = 16
MODULUS = 65521.0
INVERSE = 1.0 / MODULUS
MAGIC = 12582912.0
CHUNKS = 4
WIDE = 512
PACKED = 1024


def rounded(x):
    return (x + MAGIC) - MAGIC


def centred(x):
    return x - MODULUS * rounded(x * INVERSE)


def limbs(x):
    high = rounded(x * (1.0 / 256.0))
    return high, x - 256.0 * high


def bf16_limbs(x):
    high, low = limbs(x)
    return high.astype(jnp.bfloat16), low.astype(jnp.bfloat16)


def dot(a, b):
    return jnp.dot(a, b, preferred_element_type=jnp.float32)


def folded(x):
    quotient = rounded(x * (1.0 / 256.0))
    return 15.0 * quotient + 256.0 * (x - 256.0 * quotient)


def mul_mod(left, right):
    ah, al = bf16_limbs(left)
    bh, bl = bf16_limbs(right)
    high = centred(dot(ah, bh))
    cross = dot(jnp.concatenate([ah, al], axis=1), jnp.concatenate([bl, bh], axis=0))
    return centred(15.0 * high + folded(cross) + dot(al, bl))


def near_zero(x):
    return jnp.where(x > 32760.0, x - MODULUS, x)


def span(bits):
    masks = [0]
    for bit in bits:
        masks = masks + [m | bit for m in masks]
    return sorted(masks)


class Role:
    def __init__(self, first, second):
        self.first = first
        self.second = second
        self.gathered = span([1] + first)
        self.reduced = span([1] + second)


def call(kernel, grid, inputs, in_specs, outputs, out_specs, scratch=(), prefetch=0, aliases=None, cost=None, vmem=None):
    flops, moved = cost or (0, 0)
    return pl.pallas_call(
        kernel,
        out_shape=outputs,
        grid_spec=pltpu.PrefetchScalarGridSpec(
            num_scalar_prefetch=prefetch,
            grid=grid,
            in_specs=in_specs,
            out_specs=out_specs,
            scratch_shapes=list(scratch),
        ),
        input_output_aliases=aliases or {},
        compiler_params=pltpu.CompilerParams(
            dimension_semantics=("arbitrary",) * len(grid), vmem_limit_bytes=vmem or 48 * 1024 * 1024
        ),
        cost_estimate=pl.CostEstimate(flops=flops, bytes_accessed=moved, transcendentals=0),
    )(*inputs)


def f32(*shape):
    return jax.ShapeDtypeStruct(shape, jnp.float32)


def prepare_kernel(slots, pos, tiles, dest, t0, t1, tp, m0, m1, mp, l0, l1, lp, order_out, near_out, panel_out):
    rows = dest.shape[1]
    mine = pos[0]
    to_row = dest[...] ^ mine
    across = jnp.broadcast_to(to_row.astype(jnp.float32), (rows, rows))
    down = across.T
    earlier = lax.broadcasted_iota(jnp.int32, (rows, rows), 0) < lax.broadcasted_iota(jnp.int32, (rows, rows), 1)
    before = jnp.where((across == down) & earlier, 1.0, 0.0)
    landing = jnp.sum(before, axis=0, keepdims=True)
    place = to_row * MAX_PER_DEST + landing.astype(jnp.int32)
    choose = lax.broadcasted_iota(jnp.int32, (slots, rows), 0) == place
    order = jnp.where(choose, 1.0, 0.0).astype(jnp.bfloat16)
    order_out[...] = order

    def placed(block):
        high, low = bf16_limbs(block)
        return 256.0 * dot(order, high) + dot(order, low)

    lrows = 2 * l0.shape[1]
    near_out[:slots, :TILE] = placed(t0[...] * m0[...])
    near_out[:slots, TILE:] = placed(t1[...] * m1[...])
    near_out[slots:, :TILE] = l0[...].reshape(lrows, TILE)
    near_out[slots:, TILE:] = l1[...].reshape(lrows, TILE)
    panel_out[:slots, :] = placed(tp[...] * mp[...])
    panel_out[slots:, :] = lp[...].reshape(lrows, PANEL)


def prepare(pos, tiles, dest, thin, mask, leads, slots):
    rows, width = thin.shape
    per = width // TILE
    lper = leads.shape[1]
    total = slots + 2 * lper
    tile = lambda k: (lambda i, pos, tiles: (0, lax.rem(tiles[k], per)))
    tile3 = lambda k: (lambda i, pos, tiles: (0, 0, lax.rem(tiles[k], per)))
    zero = lambda i, pos, tiles: (0, 0)
    zero3 = lambda i, pos, tiles: (0, 0, 0)
    return call(
        functools.partial(prepare_kernel, slots),
        (1,),
        (pos, tiles, dest, thin, thin, thin, mask, mask, mask, leads, leads, leads),
        [
            pl.BlockSpec((1, rows), zero),
            pl.BlockSpec((rows, TILE), tile(0)),
            pl.BlockSpec((rows, TILE), tile(1)),
            pl.BlockSpec((rows, PANEL), zero),
            pl.BlockSpec((1, TILE), tile(0)),
            pl.BlockSpec((1, TILE), tile(1)),
            pl.BlockSpec((1, PANEL), zero),
            pl.BlockSpec((2, lper, TILE), tile3(0)),
            pl.BlockSpec((2, lper, TILE), tile3(1)),
            pl.BlockSpec((2, lper, PANEL), zero3),
        ],
        (jax.ShapeDtypeStruct((slots, rows), jnp.bfloat16), f32(total, 2 * TILE), f32(total, PANEL)),
        (
            pl.BlockSpec((slots, rows), zero),
            pl.BlockSpec((total, 2 * TILE), zero),
            pl.BlockSpec((total, PANEL), zero),
        ),
        prefetch=2,
        cost=(2 * slots * rows * 768 * 2, 4 * total * 768 * 2),
    )


def choose_kernel(cols, per, half, pos, tiles, *refs):
    near, panel, (first, second) = refs[:cols], refs[cols : 2 * cols], refs[2 * cols :]
    here = pos[1]

    def chosen(parts, owner):
        value = parts[0]
        for mask in range(1, len(parts)):
            value = jnp.where((owner ^ here) == mask, parts[mask], value)
        return value

    for k in range(2):
        columns = slice(k * TILE, (k + 1) * TILE)
        first[:, columns] = chosen([r[:, columns] for r in near], tiles[k] // per)
    rest = half - 2 * TILE
    first[:, 2 * TILE :] = chosen([r[:, :rest] for r in panel], 0)
    second[...] = chosen([r[:, rest:] for r in panel], 0)


def choose(pos, tiles, near, panel, per):
    cols = len(near)
    total = near[0].shape[0]
    half = (2 * TILE + PANEL) // 2
    zero = lambda i, pos, tiles: (0, 0)
    return call(
        functools.partial(choose_kernel, cols, per, half),
        (1,),
        (pos, tiles, *near, *panel),
        [pl.BlockSpec((total, 2 * TILE), zero)] * cols + [pl.BlockSpec((total, PANEL), zero)] * cols,
        (f32(total, half), f32(total, half)),
        (pl.BlockSpec((total, half), zero),) * 2,
        prefetch=2,
        cost=(0, 4 * total * 768 * (cols + 1)),
    )


def multiplier_kernel(n, roles, pos, *refs):
    x1, x1s, x2, x2s, g1, g1s, g2, g2s, reciprocals, lead = refs[:10]
    outs, (held, coefficient, lead_limbs) = refs[10:-3], refs[-3:]
    step = pl.program_id(0)
    mine = pos[0]
    slots = n * MAX_PER_DEST
    lper = TILE // n
    bits = n.bit_length() - 1

    @pl.when(step == 0)
    def _():
        for mask in range(n):
            plain, turned = mask >> 1, (mask >> 2) | (((mask >> 1) & 1) << (bits - 2))
            a = (g1s if mask & 1 else g1)[plain]
            b = (g2s if mask & 1 else g2)[turned]
            block = near_zero(jnp.concatenate([a, b], axis=1))
            at = pl.multiple_of((mine ^ mask) * lper, lper)
            for pivot in range(2):
                held[pivot, pl.ds(at, lper), :] = block[pivot * lper : (pivot + 1) * lper]
        high, low = bf16_limbs(near_zero(lead[...]))
        lead_limbs[0] = high
        lead_limbs[1] = low

    odd = (step & 1) == 1
    left = near_zero(jnp.where(odd, x1s[0], x1[0]))
    right = near_zero(jnp.where(odd, x2s[0], x2[0]))
    here = jnp.concatenate([left, right], axis=1)
    f0 = mul_mod(here[:, :TILE], near_zero(reciprocals[0]))
    changed = centred(here[:, TILE : 2 * TILE] - mul_mod(f0, held[0, :, TILE : 2 * TILE]))
    f1 = mul_mod(changed, near_zero(reciprocals[1]))
    both = jnp.concatenate([f0, f1], axis=1)
    panel_rows = jnp.concatenate([held[0, :, 2 * TILE :], held[1, :, 2 * TILE :]], axis=0)
    cleared = centred(here[:, 2 * TILE :] - mul_mod(both, panel_rows))
    ah, al = bf16_limbs(cleared)
    bh, bl = lead_limbs[0], lead_limbs[1]
    high = centred(dot(ah, bh))
    cross = dot(ah, bl) + dot(al, bh)
    lower = centred(15.0 * high + folded(cross) + dot(al, bl))
    coefficient[step, :, : 2 * TILE] = -both
    coefficient[step, :, 2 * TILE :] = -lower

    @pl.when(step == n - 1)
    def _():
        columns = 2 * TILE + PANEL
        sper = PANEL // n
        each = 2 * lper + sper
        for number, role in enumerate(roles):
            low_out, high_out, shift_out = outs[3 * number : 3 * number + 3]
            depth = len(role.gathered) * each
            at = lax.broadcasted_iota(jnp.int32, (columns, depth), 1)
            row = lax.broadcasted_iota(jnp.int32, (columns, depth), 0)
            wanted = jnp.zeros((columns, depth), jnp.int32)
            for k, mask in enumerate(role.gathered):
                inside = at - k * each
                owner = mine ^ mask
                source = jnp.where(
                    inside < lper,
                    owner * lper + inside,
                    jnp.where(
                        inside < 2 * lper,
                        TILE + owner * lper + (inside - lper),
                        2 * TILE + owner * sper + (inside - 2 * lper),
                    ),
                )
                wanted = jnp.where((inside >= 0) & (inside < each), source, wanted)
            select = jnp.where(row == wanted, 1.0, 0.0).astype(jnp.bfloat16)
            for k, e in enumerate(role.reduced):
                blocks = []
                for r in range(n):
                    rows = slice(r * MAX_PER_DEST, (r + 1) * MAX_PER_DEST)
                    blocks.append(coefficient[e ^ r, rows, :])
                value = jnp.concatenate(blocks, axis=0)
                high, low = bf16_limbs(value)
                scaled = centred(256.0 * value)
                scaled_high, scaled_low = bf16_limbs(scaled)
                place = slice(k * slots, (k + 1) * slots)
                picked_low, picked_high = dot(low, select), dot(high, select)
                low_out[place, :depth] = picked_low.astype(jnp.bfloat16)
                low_out[place, depth:] = dot(scaled_low, select).astype(jnp.bfloat16)
                high_out[place, :depth] = picked_high.astype(jnp.bfloat16)
                high_out[place, depth:] = dot(scaled_high, select).astype(jnp.bfloat16)
                total = jnp.sum(picked_low + 256.0 * picked_high, axis=1, keepdims=True)
                shift = centred(256.0 * centred(128.0 * centred(total)))
                shift_out[place, :] = jnp.broadcast_to(shift, (slots, TILE))


def multipliers(pos, n, roles, x1, x1s, x2, x2s, reciprocals, lead):
    slots = n * MAX_PER_DEST
    lper = TILE // n
    bits = n.bit_length() - 1
    half = (2 * TILE + PANEL) // 2
    each = 2 * lper + PANEL // n
    plain = lambda g, pos: (g >> 1, 0, 0)
    turned = lambda g, pos: ((g >> 2) | (((g >> 1) & 1) << (bits - 2)), 0, 0)
    lines = lambda g, pos: (0, slots // (2 * lper), 0)
    thin = lambda index: pl.BlockSpec((1, slots, half), index)
    lead_rows = pl.BlockSpec((n // 2, 2 * lper, half), lines)
    outputs, specs = [], []
    for role in roles:
        rows, depth = len(role.reduced) * slots, len(role.gathered) * each
        outputs += [
            jax.ShapeDtypeStruct((rows, 2 * depth), jnp.bfloat16),
            jax.ShapeDtypeStruct((rows, 2 * depth), jnp.bfloat16),
            f32(rows, TILE),
        ]
        specs += [pl.BlockSpec(o.shape, lambda g, pos: (0, 0)) for o in outputs[-3:]]
    out = call(
        functools.partial(multiplier_kernel, n, roles),
        (n,),
        (pos, x1, x1s, x2, x2s, x1, x1s, x2, x2s, reciprocals, lead),
        [thin(plain), thin(plain), thin(turned), thin(turned)]
        + [lead_rows] * 4
        + [
            pl.BlockSpec(reciprocals.shape, lambda g, pos: (0, 0, 0)),
            pl.BlockSpec(lead.shape, lambda g, pos: (0, 0)),
        ],
        tuple(outputs),
        tuple(specs),
        scratch=[
            pltpu.VMEM((2, TILE, 2 * TILE + PANEL), jnp.float32),
            pltpu.VMEM((n, slots, 2 * TILE + PANEL), jnp.float32),
            pltpu.VMEM((2, PANEL, PANEL), jnp.bfloat16),
        ],
        prefetch=1,
        cost=(8 * n * slots * PANEL * PANEL, 8 * n * slots * 768),
    )
    return [out[3 * k : 3 * k + 3] for k in range(len(roles))]


def lines_kernel(pos, leads, strip, out):
    lper, sper = leads.shape[1], strip.shape[0]
    out[:lper, :] = leads[0]
    out[lper : 2 * lper, :] = leads[1]
    out[2 * lper : 2 * lper + sper, :] = strip[...]


def column_of(chunk, half, count):
    return lambda t, pos: (2 * chunk + ((pos[0] & 1) ^ half)) * count + t


def pack_lines(pos, chunk, half, size, leads, strip):
    lper, sper = leads.shape[1], strip.shape[0]
    wide = min(PACKED, size)
    count = size // wide
    total = 2 * lper + sper
    column = column_of(chunk, half, count)
    return call(
        lines_kernel,
        (count,),
        (pos, leads, strip),
        [
            pl.BlockSpec((2, lper, wide), lambda t, pos: (0, 0, column(t, pos))),
            pl.BlockSpec((sper, wide), lambda t, pos: (0, column(t, pos))),
        ],
        f32(total, size),
        pl.BlockSpec((total, wide), lambda t, pos: (0, t)),
        prefetch=1,
        cost=(0, 8 * size * total),
    )


def thin_kernel(role, half, pos, order, thin, mask, *outs):
    high, low = bf16_limbs(thin[...] * mask[...])
    placed = 256.0 * dot(order[...], high) + dot(order[...], low)
    for out, m in zip(outs, [m for m in role.gathered if m & 1 == half]):
        for i, e in enumerate(role.reduced):
            r = (e ^ m) * MAX_PER_DEST
            at = i * MAX_PER_DEST
            out[at : at + MAX_PER_DEST, :] = placed[r : r + MAX_PER_DEST]


def pack_thin(pos, n, role, chunk, half, size, order, thin, mask):
    rows = thin.shape[0]
    slots = n * MAX_PER_DEST
    wide = min(PACKED, size)
    count = size // wide
    total = len(role.reduced) * MAX_PER_DEST
    sent = len(role.gathered) // 2
    column = column_of(chunk, half, count)
    return call(
        functools.partial(thin_kernel, role, half),
        (count,),
        (pos, order, thin, mask),
        [
            pl.BlockSpec((slots, rows), lambda t, pos: (0, 0)),
            pl.BlockSpec((rows, wide), lambda t, pos: (0, column(t, pos))),
            pl.BlockSpec((1, wide), lambda t, pos: (0, column(t, pos))),
        ],
        (f32(total, size),) * sent,
        (pl.BlockSpec((total, wide), lambda t, pos: (0, t)),) * sent,
        prefetch=1,
        cost=(4 * slots * rows * size, 4 * size * (rows + total * sent)),
    )


def partial_kernel(n, role, pos, low, high, shift, leads, strip, *refs):
    count = len(role.gathered)
    lines, thins, outs = refs[: count - 1], refs[count - 1 : 2 * count - 1], refs[2 * count - 1 :]
    slots = n * MAX_PER_DEST
    rows_of = [leads[0], leads[1], strip[...]] + [m[...] for m in lines]
    line_high, line_low = bf16_limbs(jnp.concatenate(rows_of, axis=0) - 32768.0)
    stacked = jnp.concatenate([line_low, line_high], axis=0)
    for k, e in enumerate(role.reduced):
        place = slice(k * slots, (k + 1) * slots)
        value = dot(low[place, :], stacked) + folded(dot(high[place, :], stacked)) + shift[place, :1]
        for r in range(n):
            rows = slice(r * MAX_PER_DEST, (r + 1) * MAX_PER_DEST)
            block = value[rows]
            if (r ^ e) in role.gathered:
                source = thins[role.gathered.index(r ^ e)]
                at = k * MAX_PER_DEST
                block = block + source[at : at + MAX_PER_DEST, :]
            outs[k][rows, :] = centred(block)


def partial_sums(pos, n, role, chunk, matrices, leads, strip, lines, thins):
    low, high, shift = matrices
    lper, sper = leads.shape[1], strip.shape[0]
    total, size = lines[0].shape
    slots = n * MAX_PER_DEST
    wide = min(WIDE, size)
    count = size // wide
    fixed = lambda t, pos: (0, 0)
    moving = lambda t, pos: (0, t)
    column = lambda t, pos: (2 * chunk + (pos[0] & 1)) * count + t
    return call(
        functools.partial(partial_kernel, n, role),
        (count,),
        (pos, low, high, shift, leads, strip, *lines, *thins),
        [pl.BlockSpec(a.shape, fixed) for a in matrices]
        + [
            pl.BlockSpec((2, lper, wide), lambda t, pos: (0, 0, column(t, pos))),
            pl.BlockSpec((sper, wide), lambda t, pos: (0, column(t, pos))),
        ]
        + [pl.BlockSpec((a.shape[0], wide), moving) for a in (*lines, *thins)],
        tuple(f32(slots, size) for _ in role.reduced),
        tuple(pl.BlockSpec((slots, wide), moving) for _ in role.reduced),
        prefetch=1,
        cost=(
            4 * low.shape[0] * low.shape[1] * size,
            4 * size * (total * len(thins) + thins[0].shape[0] * len(thins) + slots * len(role.reduced)),
        ),
    )


def finish_kernel(n, pos, *refs):
    parts, out = refs[:-1], refs[-1]
    mine = pos[0]
    value = parts[0][...]
    for part in parts[1:]:
        value = value + part[...]
    value = centred(value)
    value = jnp.where(value < 0.0, value + MODULUS, value) * INVERSE
    for r in range(n):
        at = pl.multiple_of((mine ^ r) * MAX_PER_DEST, MAX_PER_DEST)
        out[pl.ds(at, MAX_PER_DEST), :] = value[r * MAX_PER_DEST : (r + 1) * MAX_PER_DEST]


def finish_next(n, pos, *refs):
    finish_kernel(n, pos, *refs[:-2], refs[-1])


def finish(pos, n, chunk, half, width, parts, so_far):
    slots, size = parts[0].shape
    wide = min(2 * WIDE, size)
    count = size // wide
    inputs, specs = [pos, *parts], [pl.BlockSpec((slots, wide), lambda t, pos: (0, t))] * len(parts)
    aliases, kernel = {}, finish_kernel
    if so_far is not None:
        aliases, kernel = {len(inputs): 0}, finish_next
        inputs.append(so_far)
        specs.append(pl.BlockSpec(memory_space=pl.ANY))
    return call(
        functools.partial(kernel, n),
        (count,),
        inputs,
        specs,
        f32(slots, width),
        pl.BlockSpec((slots, wide), lambda t, pos: (0, (2 * chunk + ((pos[0] & 1) ^ half)) * count + t)),
        prefetch=1,
        aliases=aliases,
        cost=(0, 4 * size * slots * (len(parts) + 1)),
    )


def exchange(value, axis, mask):
    size = lax.axis_size(axis)
    return lax.ppermute(value, axis, [(i, i ^ mask) for i in range(size)])


def local(
    thin_line_values,
    occupied_patch_flags,
    leader_vertical_patch,
    leader_square_lines,
    leader_square_reciprocals,
    remaining_destination_line,
    leading_square_lines,
    leading_square_reciprocal,
):
    n, cols = lax.axis_size("row"), lax.axis_size("col")
    rows, width = thin_line_values.shape
    slots = n * MAX_PER_DEST
    bits = [1 << k for k in range(1, n.bit_length() - 1)]
    roles = [Role(bits[:1], bits[1:]), Role(bits[1:], bits[:1])]
    size = width // (2 * CHUNKS)
    pos = jnp.stack([lax.axis_index("row"), lax.axis_index("col")]).astype(jnp.int32)

    lines, thins = [], []
    for chunk in range(CHUNKS):
        role = roles[chunk % 2]
        come = {}
        for half in range(2):
            packed = pack_lines(pos, chunk, half, size, leader_square_lines, leading_square_lines)
            come.update({m: exchange(packed, "row", m) for m in role.gathered[1:] if m & 1 == half})
        lines.append([come[m] for m in role.gathered[1:]])

    mask = jnp.broadcast_to(
        occupied_patch_flags.astype(jnp.float32)[:, :, None], (rows // TILE, width // TILE, TILE)
    ).reshape(rows // TILE, width)
    order, near, panel = prepare(
        pos,
        leader_vertical_patch,
        remaining_destination_line.reshape(1, rows),
        thin_line_values,
        mask,
        leader_square_lines,
        slots,
    )
    panels = [panel] + [lax.ppermute(panel, "col", [(0, m)]) for m in range(1, cols)]
    nears = [near] + [exchange(near, "col", m) for m in range(1, cols)]
    for chunk in range(CHUNKS):
        role = roles[chunk % 2]
        come = {}
        for half in range(2):
            packed = pack_thin(pos, n, role, chunk, half, size, order, thin_line_values, mask)
            for m, value in zip([m for m in role.gathered if m & 1 == half], packed):
                come[m] = exchange(value, "row", m) if m else value
        thins.append([come[m] for m in role.gathered])

    stacks = [v[None] for v in choose(pos, leader_vertical_patch, nears, panels, width // TILE)]
    paths = [r.first + r.second for r in roles]
    for step in range(len(paths[0])):
        come = [exchange(stack, "row", path[step]) for stack, path in zip(stacks, paths)]
        stacks = [jnp.concatenate(pair, axis=0) for pair in zip(stacks, come)]
    gathered = []
    for stack in stacks:
        gathered += [stack, exchange(stack, "row", 1)]
    matrices = multipliers(pos, n, roles, *gathered, leader_square_reciprocals, leading_square_reciprocal)

    result = None
    for chunk in range(CHUNKS):
        role = roles[chunk % 2]
        sums = partial_sums(
            pos,
            n,
            role,
            chunk,
            matrices[chunk % 2],
            leader_square_lines,
            leading_square_lines,
            lines[chunk],
            thins[chunk],
        )
        parts = [sums[0]] + [exchange(v, "row", e) for v, e in zip(sums[1:], role.reduced[1:])]
        for half in range(2):
            chosen = [v for v, e in zip(parts, role.reduced) if e & 1 == half]
            result = finish(pos, n, chunk, half, width, chosen, result)
    return result


def solution(mesh):
    return jax.shard_map(
        local,
        mesh=mesh,
        in_specs=(
            P("row", "col"),
            P("row", "col"),
            P(),
            P(None, "row", "col"),
            P(),
            P("row"),
            P("row", "col"),
            P(),
        ),
        out_specs=P("row", "col"),
        check_vma=False,
    )
```
